32 devices in a mesh: dp: 8 (over z, y), tensor: 4 (over x, core).
Axes of the slice: x: 2, y: 2, z: 4, core: 2. Of those that a mesh axis runs over, the one named last changes fastest.
Arguments:
- tokens: bfloat16 [8, 2048, 2048], P(None, 'dp', 'tensor'), may hold values from -6 to 6
- cotangent: bfloat16 [8, 2048, 2048], P(None, 'dp', 'tensor'), may hold values from -6 to 6
- lengths: int32 [8], replicated, may hold values from 1 to 2048, 9830 in all
- w_query: bfloat16 [2048, 2048], P(None, 'tensor'), may hold values from -0.125 to 0.125
- w_key: bfloat16 [2048, 2048], P(None, 'tensor'), may hold values from -0.125 to 0.125
- w_value: bfloat16 [2048, 2048], P(None, 'tensor'), may hold values from -0.125 to 0.125
- w_gate: bfloat16 [2048, 2048], P(None, 'tensor'), may hold values from -0.125 to 0.125
- w_out: bfloat16 [2048, 2048], P('tensor'), may hold values from -0.125 to 0.125
- w_glu_in: bfloat16 [2048, 2, 5632], P(None, None, 'tensor'), may hold values from -0.125 to 0.125
- w_glu_out: bfloat16 [5632, 2048], P('tensor'), may hold values from -0.078125 to 0.078125
Outputs:
- output: bfloat16 [8, 2048, 2048], P(None, 'dp', 'tensor')
- input_grad: bfloat16 [8, 2048, 2048], P(None, 'dp', 'tensor')
- grad_query: float32 [2048, 2048], P('dp', 'tensor')
- grad_key: float32 [2048, 2048], P('dp', 'tensor')
- grad_value: float32 [2048, 2048], P('dp', 'tensor')
- grad_gate: float32 [2048, 2048], P('dp', 'tensor')
- grad_out: float32 [2048, 2048], P('tensor', 'dp')
- grad_glu_in: float32 [2048, 2, 5632], P('dp', None, 'tensor')
- grad_glu_out: float32 [5632, 2048], P('tensor', 'dp')
- rms_values: float32 [3], replicated
The draws below stay inside these ranges and needn't reach their ends.
Inputs may be any that keep to these rules, and one draw needn't show every extreme that they name: Every sequence has at least one valid token and the longest has exactly 2048; the lengths add up to three fifths of 16384, rounded down.
All inputs are finite; a program needn't handle non-finite values.
Results may differ from the reference program's by a relative error of at most 0.019.
Values may be sent and summed in bfloat16 or wider, within the bound.
No kernel may reach another device: no remote copies, remote signals or barrier semaphores. Data moves between devices by JAX's collectives and lax.ppermute only.
A program may use at most 320 MiB of HBM per device.

```python
import math
import jax
import jax.numpy as jnp
import numpy as np
from jax import lax

D = 2048
HEADS = 16
HEAD_DIM = 128
FF = 5632
BLOCK = 256
LMAX = 2048
SEQS = 8


def levels(stream_key, dims, split, least, high):
    loudness, own = 1.0, jax.random.fold_in(stream_key, 6)
    for position, parts in split:
        steps = jnp.exp(jax.random.uniform(jax.random.fold_in(own, position), (parts,), jnp.float32, least / len(split), high / len(split)))
        loudness = loudness * jnp.repeat(steps, dims[position] // parts).reshape([-1 if axis == position else 1 for axis in range(len(dims))])
    return loudness


def split_up(count, total, reach, slope):
    loads = [(1 << 20) // math.isqrt(rank ** slope) + 1 for rank in range(2, count + 1)]
    surplus, given = total - reach - (count - 1), [1] * (count - 1)
    while surplus > 0:
        candidates = [i for i in range(count - 1) if given[i] < reach]
        whole, budget = sum([loads[i] for i in candidates]), surplus
        for i in candidates:
            more = min(reach - given[i], max(1, budget * loads[i] // whole), surplus)
            given[i] = given[i] + more
            surplus = surplus - more
    return np.array([reach] + given)


def uneven(rng, amount, total, most, skew):
    if amount == 2:
        one = jax.random.randint(rng, (), max(1, total - most), min(most, total - 1) + 1)
        return jnp.stack([one, total - one])
    sizes = jnp.asarray(split_up(amount, total, most, skew), jnp.int32)
    couples = (amount - 1) // 2
    source_of, receiver = sizes[1:1 + 2 * couples:2], sizes[2:2 + 2 * couples:2]
    room = jnp.minimum(source_of - 1, most - receiver)
    passed = jax.random.randint(jax.random.fold_in(rng, 1), (couples,), 0, 1 << 20) % (room + 1)
    sizes = sizes.at[1:1 + 2 * couples:2].set(source_of - passed).at[2:2 + 2 * couples:2].set(receiver + passed)
    return sizes[jax.random.permutation(jax.random.fold_in(rng, 2), amount)]


def bell_draw(rng, shape, deviation, reach, pieces=(), kind=jnp.bfloat16):
    entries = jax.random.normal(rng, shape, jnp.float32) * deviation
    if len(pieces) > 0:
        entries = levels(rng, shape, pieces, -0.22, 0.18) * entries
    return jnp.clip(entries, min=-reach, max=reach).astype(kind)


def setup_inputs(seed: int = 0) -> dict:
    streams_of = jax.random.split(jax.random.key(seed), 11)
    return {
        "tokens": bell_draw(streams_of[0], (SEQS, LMAX, D), 1.0, 6.0, ((1, 8), (2, 4))),
        "cotangent": bell_draw(streams_of[1], (SEQS, LMAX, D), 1.0, 6.0, ((1, 8), (2, 4))),
        "lengths": uneven(streams_of[2], SEQS, SEQS * LMAX * 3 // 5, LMAX, 1).astype(jnp.int32),
        "w_query": bell_draw(streams_of[3], (D, D), D ** -0.5, 0.125, ((1, 4),)),
        "w_key": bell_draw(streams_of[4], (D, D), D ** -0.5, 0.125, ((1, 4),)),
        "w_value": bell_draw(streams_of[5], (D, D), D ** -0.5, 0.125, ((1, 4),)),
        "w_gate": bell_draw(streams_of[6], (D, D), D ** -0.5, 0.125, ((1, 4),)),
        "w_out": bell_draw(streams_of[7], (D, D), D ** -0.5, 0.125, ((0, 4),)),
        "w_glu_in": bell_draw(streams_of[8], (D, 2, FF), D ** -0.5, 0.125, ((2, 4),)),
        "w_glu_out": bell_draw(streams_of[9], (FF, D), FF ** -0.5, 0.078125, ((0, 4),)),
    }


EPSILON = 1e-06
HIGHEST = lax.Precision.HIGHEST

@jax.custom_vjp
def low(v):
    return lax.optimization_barrier(v.astype(jnp.bfloat16)).astype(jnp.float32)

@jax.custom_vjp
def low_back(v):
    return v

def low_keep(v):
    return (low(v), None)

def low_pass(kept, grad):
    return (grad,)

def back_keep(v):
    return (v, None)

def back_low(kept, grad):
    return (low(grad),)
low.defvjp(low_keep, low_pass)
low_back.defvjp(back_keep, back_low)

def matmul(left, right):
    return jnp.dot(left, right, precision=HIGHEST, preferred_element_type=jnp.float32)

def normalize(values):
    return values * lax.rsqrt(lax.optimization_barrier(jnp.mean(values * values, axis=-1, keepdims=True)) + EPSILON)

def decay_tables():
    head_ids = jnp.arange(HEADS).astype(jnp.float32)
    slopes = jnp.exp2(-8.0 * (head_ids + 1.0) / HEADS)
    places = jnp.arange(BLOCK).astype(jnp.float32)
    distance = places[:, None] - places[None, :]
    inside = jnp.where(distance >= 0, jnp.exp(-slopes[:, None, None] * jnp.maximum(distance, 0.0)), 0.0)
    start_decay = jnp.exp(-slopes[None, :] * (places[:, None] + 1.0))
    finish = jnp.exp(-slopes[None, :] * (BLOCK - 1.0 - places[:, None]))
    carry_decay = jnp.exp(-slopes * BLOCK)
    return (inside, start_decay, finish, carry_decay)

def lightning(queries, key_rows, value_rows, tables):
    inside, start_decay, finish, carry_decay = tables
    block_shape = (queries.shape[0] // BLOCK, BLOCK, HEADS, HEAD_DIM)

    def advance(carried, blocks_in):
        query_block, key_block, value_block = blocks_in
        raw_scores = low_back(jnp.einsum('ihd,jhd->hij', query_block, key_block, precision=HIGHEST))
        weights = low(raw_scores * inside)
        near_part = jnp.einsum('hij,jhd->ihd', weights, value_block, precision=HIGHEST)
        far_part = low_back(jnp.einsum('ihd,hde->ihe', query_block, low(carried), precision=HIGHEST))
        keyed_rows = low(key_block * finish[:, :, None])
        update = low_back(jnp.einsum('jhd,jhe->hde', keyed_rows, value_block, precision=HIGHEST))
        return (carry_decay[:, None, None] * carried + update, near_part + far_part * start_decay[:, :, None])
    initial = jnp.zeros((HEADS, HEAD_DIM, HEAD_DIM), dtype=jnp.float32)
    blocks_in = (queries.reshape(block_shape), key_rows.reshape(block_shape), value_rows.reshape(block_shape))
    final_state, mixed_blocks = lax.scan(jax.checkpoint(advance), initial, blocks_in)
    return mixed_blocks.reshape(queries.shape[0], HEADS * HEAD_DIM)

def layer(inputs, validity, params, tables):
    w_query, w_key, w_value, w_gate, w_out, w_glu_in, w_glu_out = params
    normed_one = low(normalize(inputs))
    query_pre = low_back(matmul(normed_one, w_query))
    key_pre = low_back(matmul(normed_one, w_key))
    value_pre = low_back(matmul(normed_one, w_value))
    gate_pre = low_back(matmul(normed_one, w_gate))
    queries = low(jax.nn.silu(query_pre))
    key_rows = low(jax.nn.silu(key_pre))
    value_rows = low(value_pre)
    head_shape = (inputs.shape[0], HEADS, HEAD_DIM)
    mixture = low_back(lightning(queries.reshape(head_shape), key_rows.reshape(head_shape), value_rows.reshape(head_shape), tables))
    gated_out = low(normalize(mixture) * gate_pre)
    attn_out = low_back(matmul(gated_out, w_out))
    residual = inputs + attn_out
    normed_two = low(normalize(residual))
    both_pre = matmul(normed_two, w_glu_in.reshape(D, 2 * FF))
    gate_half = low_back(both_pre[:, :FF])
    up_half = low_back(both_pre[:, FF:])
    hidden = low(gate_half * up_half)
    glu_out = low_back(matmul(hidden, w_glu_out))
    row_mask = validity[:, None]
    output = row_mask * (residual + glu_out)
    square_sums = jnp.stack([jnp.sum(row_mask * residual * residual), jnp.sum(row_mask * attn_out * attn_out), jnp.sum(row_mask * glu_out * glu_out)])
    return (output, square_sums)

def reference(tokens, cotangent, lengths, w_query, w_key, w_value, w_gate, w_out, w_glu_in, w_glu_out):
    tables = decay_tables()
    weights = tuple((matrix.astype(jnp.float32) for matrix in (w_query, w_key, w_value, w_gate, w_out, w_glu_in, w_glu_out)))
    positions = jnp.arange(LMAX, dtype=jnp.int32)
    validity = (positions[None, :] < lengths[:, None]).astype(jnp.float32)

    def forward(inputs, params):

        def one_sequence(pair_in):
            return layer(pair_in[0], pair_in[1], params, tables)
        outputs, square_sums = lax.map(jax.checkpoint(one_sequence), (inputs, validity))
        return (outputs, lax.optimization_barrier(jnp.sum(square_sums, axis=0)))
    outputs, pullback, totals = jax.vjp(forward, tokens.astype(jnp.float32), weights, has_aux=True)
    input_grad, weight_grads = pullback(cotangent.astype(jnp.float32))
    token_count = jnp.sum(lengths).astype(jnp.float32)
    rms_values = jnp.sqrt(totals / (token_count * D) + EPSILON)
    return (outputs.astype(jnp.bfloat16), input_grad.astype(jnp.bfloat16), weight_grads[0], weight_grads[1], weight_grads[2], weight_grads[3], weight_grads[4], weight_grads[5], weight_grads[6], rms_values)
```

```python
import functools

import jax
import jax.numpy as jnp
from jax import lax
from jax.experimental import pallas as pl
from jax.experimental.pallas import tpu as pltpu
from jax.sharding import PartitionSpec as P

HEAD_DIM = 128
EPSILON = 1e-06
NARROW = jnp.bfloat16
FLOAT = jnp.float32
CHUNKS = 2

NN = (((1,), (0,)), ((), ()))
NT = (((1,), (1,)), ((), ()))
TN = (((0,), (0,)), ((), ()))


def mm(left, right, dims=NN):
    return lax.dot_general(left, right, dims, preferred_element_type=FLOAT)


def swap(value, axis, mask):
    size = lax.axis_size(axis)
    return lax.ppermute(value, axis, [(i, i ^ mask) for i in range(size)])


def gather_shards(value):
    size = lax.axis_size("tensor")
    shards = {0: value}
    mask = size // 2
    while mask:
        shards.update({k | mask: swap(v, "tensor", mask) for k, v in list(shards.items())})
        mask //= 2
    return [shards[k] for k in range(size)]


def scatter_terms(pieces):
    size = lax.axis_size("tensor")
    current = {k: [v] for k, v in enumerate(pieces)}
    mask = 1
    while mask < size:
        sent = {k: v for k, v in current.items() if k & mask}
        kept = {k: v for k, v in current.items() if not k & mask}
        for k, terms in sent.items():
            total = terms[0]
            if len(terms) > 1:
                total = sum(v.astype(FLOAT) for v in terms).astype(NARROW)
            kept[k ^ mask] = kept[k ^ mask] + [swap(total, "tensor", mask)]
        current = kept
        mask *= 2
    return current[0]


def total_rows(value, axes=("tensor",)):
    for axis in axes:
        mask = 1
        while mask < lax.axis_size(axis):
            value = value + swap(value, axis, mask)
            mask *= 2
    return value


def block_order(size):
    order = [0]
    while len(order) < size:
        order = [2 * k for k in order] + [2 * k + 1 for k in order]
    return order


def reduce_blocks(kept, sent):
    size = lax.axis_size("dp")
    mask = 1
    while True:
        arrived = swap(sent, "dp", mask)
        total = kept.astype(FLOAT) + arrived.astype(FLOAT)
        mask *= 2
        if mask >= size:
            return total
        half = total.shape[0] // 2
        narrow = total.astype(NARROW)
        kept, sent = narrow[:half], narrow[half:]


def to_row(column):
    wide = jnp.broadcast_to(column, (column.shape[0], 128))
    return jnp.transpose(wide)[:8]


def to_column(row):
    tall = jnp.broadcast_to(row[0:1], (128, row.shape[1]))
    return jnp.transpose(tall)[:, :1]


class Tiles:
    def __init__(self, chunk, chunks, seqs, span, group, heads):
        self.chunk, self.span, self.group, self.heads = chunk, span, group, heads
        self.rows = seqs * span
        self.chunk_seqs = seqs // chunks
        self.chunk_rows = self.chunk_seqs * span
        self.tile = group * span
        self.steps = self.chunk_seqs // group

    def spec(self, kind, shape):
        off = self.chunk * self.steps
        if kind == "rows":
            start = off if shape[0] == self.rows and self.rows != self.chunk_rows else 0
            return pl.BlockSpec((self.tile, shape[1]), lambda i, s: (start + i, 0))
        if kind == "vec":
            start = off if shape[1] == self.rows and self.rows != self.chunk_rows else 0
            return pl.BlockSpec((8, self.tile), lambda i, s: (0, start + i))
        if kind == "state":
            return pl.BlockSpec((self.group,) + tuple(shape[1:]), lambda i, s: (i, 0, 0, 0))
        zero = (0,) * len(shape)
        if kind == "acc":
            return pl.BlockSpec(tuple(shape), lambda i, s: zero)
        return pl.BlockSpec(tuple(shape), lambda i, s: zero, pipeline_mode=pl.Buffered(1))

    def call(self, name, body, scalars, ins, outs, scratch=(), flops=0):
        arrays = [a for _, a in ins]
        in_specs = [self.spec(kind, a.shape) for kind, a in ins]
        aliases, carried = {}, 0
        for n, out in enumerate(outs):
            if out[3] is not None:
                aliases[1 + len(arrays)] = n
                arrays.append(out[3])
                in_specs.append(pl.BlockSpec(memory_space=pl.ANY))
                carried += 1
        count = len(ins)

        def kernel(scalar_ref, *refs):
            first = count + carried
            body(scalar_ref, refs[:count], refs[first : first + len(outs)], refs[first + len(outs) :])

        moved = sum(self.tile * self.steps * 2 * 512 for _ in arrays)
        return pl.pallas_call(
            kernel,
            name=name,
            out_shape=[jax.ShapeDtypeStruct(o[1], o[2]) for o in outs],
            grid_spec=pltpu.PrefetchScalarGridSpec(
                num_scalar_prefetch=1,
                grid=(self.steps,),
                in_specs=in_specs,
                out_specs=[self.spec(o[0], o[1]) for o in outs],
                scratch_shapes=list(scratch),
            ),
            input_output_aliases=aliases,
            compiler_params=pltpu.CompilerParams(vmem_limit_bytes=60 * 1024 * 1024),
            cost_estimate=pl.CostEstimate(flops=int(flops), bytes_accessed=int(moved), transcendentals=0),
        )(scalars, *arrays)


def lanes(start, width):
    return pl.ds(pl.multiple_of(start, 128), width)


def valid_column(scalar_ref, tiles, piece):
    seq = tiles.chunk * tiles.chunk_seqs + pl.program_id(0) * tiles.group + piece
    place = lax.broadcasted_iota(jnp.int32, (tiles.span, 1), 0) + scalar_ref[1] * tiles.span
    return (place < scalar_ref[2 + seq]).astype(FLOAT)


def silu_slope(values):
    part = jax.nn.sigmoid(values)
    return part * (1.0 + values * (1.0 - part))


def assemble(scalar_ref, shards, target, scale, width):
    for k, shard in enumerate(shards):
        rows = shard[...]
        if scale is not None:
            rows = (rows.astype(FLOAT) * scale).astype(NARROW)
        target[:, lanes((scalar_ref[0] ^ k) * width, width)] = rows


def split_blocks(scalar_ref, source, kept, sent, order):
    half = len(order) // 2
    width = source.shape[1] // len(order)
    for place, k in enumerate(order):
        target = kept if place < half else sent
        at = (place % half) * width
        target[:, at : at + width] = source[:, lanes((scalar_ref[1] ^ k) * width, width)]


def inverse_rms(shards):
    total = None
    for shard in shards:
        rows = shard[...].astype(FLOAT)
        part = jnp.sum(rows * rows, axis=1, keepdims=True)
        total = part if total is None else total + part
    width = shards[0].shape[1] * len(shards)
    return lax.rsqrt(total / width + EPSILON)


def project_body(tiles, order, scalar_ref, ins, outs, scratch):
    size = len(ins) - 7
    shards = ins[:size]
    w_query, w_key, w_value, w_gate, inside, finish, _ = ins[size:]
    kept, sent, query_pre, key_pre, gate_pre, query, key, value, near, update, inverse_row = outs
    (normed,) = scratch
    inverse = inverse_rms(shards)
    inverse_row[...] = to_row(inverse)
    assemble(scalar_ref, shards, normed, inverse, shards[0].shape[1])
    split_blocks(scalar_ref, normed, kept, sent, order)
    pre = mm(normed[...], w_query[...])
    query_pre[...] = pre
    query[...] = (pre * jax.nn.sigmoid(pre)).astype(NARROW)
    pre = mm(normed[...], w_key[...])
    key_pre[...] = pre
    key[...] = (pre * jax.nn.sigmoid(pre)).astype(NARROW)
    value[...] = mm(normed[...], w_value[...]).astype(NARROW)
    gate_pre[...] = mm(normed[...], w_gate[...])
    for piece in range(tiles.group):
        rows = slice(piece * tiles.span, (piece + 1) * tiles.span)
        for head in range(tiles.heads):
            cols = slice(head * HEAD_DIM, (head + 1) * HEAD_DIM)
            k_head, v_head = key[rows, cols], value[rows, cols]
            scores = (mm(query[rows, cols], k_head, NT) * inside[head]).astype(NARROW)
            near[rows, cols] = mm(scores, v_head)
            keyed = (k_head.astype(FLOAT) * finish[:, cols]).astype(NARROW)
            update[piece, head] = mm(keyed, v_head, TN).astype(NARROW)


def mix_body(tiles, scalar_ref, ins, outs, scratch):
    query, near, gate_pre, state, start, w_out = ins
    mixture, square_row, *pieces = outs
    width = near.shape[1]
    for piece in range(tiles.group):
        rows = slice(piece * tiles.span, (piece + 1) * tiles.span)
        for head in range(tiles.heads):
            cols = slice(head * HEAD_DIM, (head + 1) * HEAD_DIM)
            far = mm(query[rows, cols], state[piece, head])
            mixture[rows, cols] = near[rows, cols] + far * start[:, cols]
    mixed = mixture[...]
    square_row[...] = to_row(jnp.sum(mixed * mixed, axis=1, keepdims=True))
    gated = (mixed * gate_pre[...]).astype(NARROW)
    for k, target in enumerate(pieces):
        target[...] = mm(gated, w_out[:, lanes((scalar_ref[0] ^ k) * width, width)]).astype(NARROW)


def mean_inverse(row, full):
    return lax.rsqrt(to_column(row[...]) / full + EPSILON)


def residual_body(tiles, full, scalar_ref, ins, outs, scratch):
    tokens, square_row, *terms = ins
    residual, narrow, attn, sums = outs

    @pl.when(pl.program_id(0) == 0)
    def _():
        sums[...] = jnp.zeros_like(sums)

    total = sum(term[...].astype(FLOAT) for term in terms)
    branch = total * mean_inverse(square_row, full)
    attn[...] = branch
    joined = tokens[...].astype(FLOAT) + branch
    residual[...] = joined
    narrow[...] = joined.astype(NARROW)
    for piece in range(tiles.group):
        rows = slice(piece * tiles.span, (piece + 1) * tiles.span)
        valid = valid_column(scalar_ref, tiles, piece)
        sums[0:1, :] += jnp.sum(valid * joined[rows] * joined[rows], axis=0, keepdims=True)
        sums[1:2, :] += jnp.sum(valid * branch[rows] * branch[rows], axis=0, keepdims=True)


def glu_body(tiles, order, scalar_ref, ins, outs, scratch):
    size = (len(ins) - 3) // 2
    shards, cot_shards = ins[:size], ins[size : 2 * size]
    w_first, w_up, w_down = ins[2 * size :]
    kept, sent, cot_kept, cot_sent, hidden, grad_gate, grad_up, inverse_row, inner_row = outs[:9]
    glu_pieces, grad_pieces = outs[9 : 9 + size], outs[9 + size :]
    normed, cot = scratch
    width = shards[0].shape[1]
    inverse = inverse_rms(shards)
    inverse_row[...] = to_row(inverse)
    assemble(scalar_ref, shards, normed, inverse, width)
    split_blocks(scalar_ref, normed, kept, sent, order)
    valid = jnp.concatenate([valid_column(scalar_ref, tiles, piece) for piece in range(tiles.group)], axis=0)
    assemble(scalar_ref, cot_shards, cot, valid, width)
    split_blocks(scalar_ref, cot, cot_kept, cot_sent, order)
    gate_half = mm(normed[...], w_first[...])
    up_half = mm(normed[...], w_up[...])
    product = gate_half * up_half
    hidden[...] = product.astype(NARROW)
    grad_hidden = mm(cot[...], w_down[...], NT)
    inner_row[...] = to_row(2.0 * jnp.sum(grad_hidden * product, axis=1, keepdims=True))
    grad_gate[...] = (grad_hidden * up_half).astype(NARROW)
    grad_up[...] = (grad_hidden * gate_half).astype(NARROW)
    for k in range(size):
        own = lanes((scalar_ref[0] ^ k) * width, width)
        grad_pieces[k][...] = (
            mm(grad_gate[...], w_first[own, :], NT) + mm(grad_up[...], w_up[own, :], NT)
        ).astype(NARROW)
    for k in range(size):
        own = lanes((scalar_ref[0] ^ k) * width, width)
        glu_pieces[k][...] = mm(hidden[...], w_down[:, own]).astype(NARROW)


def grad_residual_body(tiles, full, scalar_ref, ins, outs, scratch):
    cot, residual, attn, inverse_row, inner_row, *terms = ins
    grad_residual, narrow, inner_mix_row = outs
    total = sum(term[...].astype(FLOAT) for term in terms)
    inverse = to_column(inverse_row[...])
    inner = to_column(inner_row[...])
    valid = jnp.concatenate([valid_column(scalar_ref, tiles, piece) for piece in range(tiles.group)], axis=0)
    normed = residual[...] * inverse
    grad = valid * cot[...].astype(FLOAT) + inverse * (total - normed * (inner / full))
    grad_residual[...] = grad
    rounded = grad.astype(NARROW)
    narrow[...] = rounded
    inner_mix_row[...] = to_row(jnp.sum(rounded.astype(FLOAT) * attn[...], axis=1, keepdims=True))


def grad_mix_body(tiles, full, order, scalar_ref, ins, outs, scratch):
    size = len(ins) - 13
    shards = ins[:size]
    (mixture, gate_pre, query_pre, query, key, value, state, square_row, inner_row, inside, start, w_out, _) = ins[size:]
    kept, sent, gated, grad_gate_pre, grad_query_pre, grad_mix, grad_state, inner_one_row = outs
    whole, grad_query = scratch
    assemble(scalar_ref, shards, whole, None, shards[0].shape[1])
    split_blocks(scalar_ref, whole, kept, sent, order)
    grad_gated = mm(whole[...], w_out[...], NT)
    inverse = mean_inverse(square_row, full)
    inner = to_column(inner_row[...])
    gate = gate_pre[...]
    normed = mixture[...] * inverse
    gated[...] = (normed * gate).astype(NARROW)
    grad_gate = (grad_gated * normed).astype(NARROW)
    grad_gate_pre[...] = grad_gate
    grad_mix[...] = (inverse * (grad_gated * gate - normed * (inner / full))).astype(NARROW)
    for piece in range(tiles.group):
        rows = slice(piece * tiles.span, (piece + 1) * tiles.span)
        for head in range(tiles.heads):
            cols = slice(head * HEAD_DIM, (head + 1) * HEAD_DIM)
            grad_head = grad_mix[rows, cols]
            grad_scores = (mm(grad_head, value[rows, cols], NT) * inside[head]).astype(NARROW)
            grad_far = (grad_head.astype(FLOAT) * start[:, cols]).astype(NARROW)
            grad_query[rows, cols] = mm(grad_scores, key[rows, cols]) + mm(grad_far, state[piece, head], NT)
            grad_state[piece, head] = mm(query[rows, cols], grad_far, TN).astype(NARROW)
    pre = query_pre[...]
    grad_pre = (grad_query[...] * silu_slope(pre)).astype(NARROW)
    grad_query_pre[...] = grad_pre
    inner_one_row[...] = to_row(
        jnp.sum(grad_pre.astype(FLOAT) * pre + grad_gate.astype(FLOAT) * gate, axis=1, keepdims=True)
    )


def grad_key_body(tiles, scalar_ref, ins, outs, scratch):
    (query, key, value, grad_mix, grad_update, key_pre, grad_query_pre, grad_gate_pre, inner_in) = ins[:9]
    inside, finish, w_query, w_key, w_value, w_gate = ins[9:]
    grad_key_pre, grad_value_pre, inner_row, *pieces = outs
    (grad_key,) = scratch
    width = key.shape[1]
    for piece in range(tiles.group):
        rows = slice(piece * tiles.span, (piece + 1) * tiles.span)
        for head in range(tiles.heads):
            cols = slice(head * HEAD_DIM, (head + 1) * HEAD_DIM)
            q_head, k_head, v_head = query[rows, cols], key[rows, cols], value[rows, cols]
            grad_head, grad_up = grad_mix[rows, cols], grad_update[piece, head]
            scores = (mm(q_head, k_head, NT) * inside[head]).astype(NARROW)
            grad_scores = (mm(grad_head, v_head, NT) * inside[head]).astype(NARROW)
            keyed = (k_head.astype(FLOAT) * finish[:, cols]).astype(NARROW)
            grad_key[rows, cols] = mm(grad_scores, q_head, TN) + mm(v_head, grad_up, NT) * finish[:, cols]
            grad_value_pre[rows, cols] = (mm(scores, grad_head, TN) + mm(keyed, grad_up)).astype(NARROW)
    pre = key_pre[...]
    grad_pre = (grad_key[...] * silu_slope(pre)).astype(NARROW)
    grad_key_pre[...] = grad_pre
    grad_value = grad_value_pre[...]
    inner = jnp.sum(
        grad_pre.astype(FLOAT) * pre + grad_value.astype(FLOAT) * value[...].astype(FLOAT), axis=1, keepdims=True
    )
    inner_row[...] = inner_in[...] + to_row(inner)
    for k, target in enumerate(pieces):
        own = lanes((scalar_ref[0] ^ k) * width, width)
        target[...] = (
            mm(grad_query_pre[...], w_query[own, :], NT)
            + mm(grad_pre, w_key[own, :], NT)
            + mm(grad_value, w_value[own, :], NT)
            + mm(grad_gate_pre[...], w_gate[own, :], NT)
        ).astype(NARROW)


def input_grad_body(tiles, full, scalar_ref, ins, outs, scratch):
    tokens, grad_residual, inverse_row, inner_row, *terms = ins
    (target,) = outs
    total = sum(term[...].astype(FLOAT) for term in terms)
    inverse = to_column(inverse_row[...])
    inner = to_column(inner_row[...])
    normed = tokens[...].astype(FLOAT) * inverse
    target[...] = (grad_residual[...] + inverse * (total - normed * (inner / full))).astype(NARROW)


def output_body(tiles, scalar_ref, ins, outs, scratch):
    residual, *terms = ins
    target, sums = outs

    @pl.when(pl.program_id(0) == 0)
    def _():
        sums[...] = jnp.zeros_like(sums)

    total = sum(term[...].astype(FLOAT) for term in terms)
    joined = residual[...] + total
    for piece in range(tiles.group):
        rows = slice(piece * tiles.span, (piece + 1) * tiles.span)
        valid = valid_column(scalar_ref, tiles, piece)
        target[rows, :] = (valid * joined[rows]).astype(NARROW)
        sums[0:1, :] += jnp.sum(valid * total[rows] * total[rows], axis=0, keepdims=True)


def scan_body(reverse, source, decay, target):
    count = source.shape[0]
    carried = jnp.zeros(source.shape[1:], FLOAT)
    for block in reversed(range(count)) if reverse else range(count):
        target[block] = carried.astype(NARROW)
        carried = decay[...] * carried + source[block].astype(FLOAT)


def share_states(update, slopes, span, reverse):
    size = lax.axis_size("dp")
    seqs, heads = update.shape[:2]
    parts = size // seqs
    group = heads // parts
    own = lax.dynamic_slice_in_dim(slopes, (lax.axis_index("dp") % parts) * group, group)
    decay = jnp.broadcast_to(jnp.exp(-own * span)[:, None, None], (group, HEAD_DIM, HEAD_DIM))
    blocks = update.reshape(size, group, HEAD_DIM, HEAD_DIM)
    arrived = lax.all_to_all(blocks, "dp", 0, 0, tiled=True)
    summed = pl.pallas_call(
        functools.partial(scan_body, reverse),
        name="scan_states",
        out_shape=jax.ShapeDtypeStruct(arrived.shape, NARROW),
    )(arrived, decay)
    returned = lax.all_to_all(summed, "dp", 0, 0, tiled=True)
    return returned.reshape(update.shape)


def local(tokens, cotangent, lengths, w_query, w_key, w_value, w_gate, w_out, w_glu_in, w_glu_out):
    seqs, span, width = tokens.shape
    dp_size, tensor_size = lax.axis_size("dp"), lax.axis_size("tensor")
    rows, full = seqs * span, width * tensor_size
    ff = w_glu_out.shape[0]
    heads = width // HEAD_DIM
    tensor_index, dp_index = lax.axis_index("tensor"), lax.axis_index("dp")
    scalars = jnp.concatenate([jnp.stack([tensor_index, dp_index]).astype(jnp.int32), lengths])
    order = block_order(dp_size)
    chunks = CHUNKS
    group = max(1, 256 // span)
    wide = seqs // chunks
    half_full = full // 2

    head_ids = (tensor_index * heads + jnp.arange(heads, dtype=jnp.int32)).astype(FLOAT)
    slopes = jnp.exp2(-8.0 * (head_ids + 1.0) / (heads * tensor_size))
    places = jnp.arange(span).astype(FLOAT)
    distance = places[:, None] - places[None, :]
    inside = jnp.where(distance >= 0, jnp.exp(-slopes[:, None, None] * jnp.maximum(distance, 0.0)), 0.0)
    lane_slopes = jnp.repeat(slopes, HEAD_DIM)
    start = jnp.exp(-lane_slopes[None, :] * (places[:, None] + 1.0))
    finish = jnp.exp(-lane_slopes[None, :] * (span - 1.0 - places[:, None]))

    token_rows = tokens.reshape(rows, width)
    cot_rows = cotangent.reshape(rows, width)
    w_first, w_up = w_glu_in[:, 0, :], w_glu_in[:, 1, :]
    tiles = [Tiles(n, chunks, seqs, span, group, heads) for n in range(chunks)]
    broad = [Tiles(n, chunks, seqs, span, wide, heads) for n in range(chunks)]
    part_rows = rows // chunks

    def cut(array, n):
        return array[n * part_rows : (n + 1) * part_rows]

    def full_outs(shapes, carried):
        return [("rows", (rows, s), NARROW, None if carried is None else carried[n]) for n, s in enumerate(shapes)]

    def part(size, dtype=FLOAT):
        return ("rows", (part_rows, size), dtype, None)

    vec = ("vec", (8, part_rows), FLOAT, None)
    pieces = [part(width, NARROW)] * tensor_size
    state_shape = ("state", (wide, heads, HEAD_DIM, HEAD_DIM), NARROW, None)

    x_shards = [gather_shards(cut(token_rows, n)) for n in range(chunks)]
    cot_shards = [gather_shards(cut(cot_rows, n)) for n in range(chunks)]
    saved = [{} for _ in range(chunks)]
    carried_one = carried_two = carried_three = carried_four = None
    sums_a = jnp.zeros((2,), FLOAT)
    for n in range(chunks):
        s = saved[n]
        out = tiles[n].call(
            "project",
            functools.partial(project_body, tiles[n], order),
            scalars,
            [("rows", v) for v in x_shards[n]]
            + [("whole", v) for v in (w_query, w_key, w_value, w_gate, inside, finish, start)],
            full_outs([half_full] * 2, carried_one)
            + [part(width)] * 3
            + [part(width, NARROW)] * 3
            + [part(width), state_shape, vec],
            [pltpu.VMEM((tiles[n].tile, full), NARROW)],
            flops=2 * part_rows * full * width * 4,
        )
        carried_one = out[:2]
        s["qz"], s["kz"], s["uz"], s["q"], s["k"], s["v"], near, update, s["inv1"] = out[2:]
        s["state"] = share_states(update, slopes, span, False)
        out = tiles[n].call(
            "mix",
            functools.partial(mix_body, tiles[n]),
            scalars,
            [("rows", s["q"]), ("rows", near), ("rows", s["uz"]), ("state", s["state"]), ("whole", start), ("whole", w_out)],
            [part(width), vec] + pieces,
            flops=2 * part_rows * full * width,
        )
        s["mix"], square = out[:2]
        s["square"] = total_rows(square)
        terms = scatter_terms(out[2:])
        s["residual"], s["narrow"], s["attn"], sums = broad[n].call(
            "residual",
            functools.partial(residual_body, broad[n], full),
            scalars,
            [("rows", token_rows), ("vec", s["square"])] + [("rows", v) for v in terms],
            [part(width), part(width, NARROW), part(width), ("acc", (8, width), FLOAT, None)],
        )
        sums_a = sums_a + jnp.sum(sums[:2], axis=1)
    sums_b = jnp.zeros((), FLOAT)
    for n in range(chunks):
        s = saved[n]
        shards = gather_shards(s["narrow"])
        out = tiles[n].call(
            "glu",
            functools.partial(glu_body, tiles[n], order),
            scalars,
            [("rows", v) for v in shards + cot_shards[n]] + [("whole", v) for v in (w_first, w_up, w_glu_out)],
            full_outs([half_full] * 4 + [ff] * 3, carried_two) + [vec, vec] + pieces + pieces,
            [pltpu.VMEM((tiles[n].tile, full), NARROW)] * 2,
            flops=2 * part_rows * full * ff * 6,
        )
        carried_two = out[:7]
        s["inv2"], inner = out[7:9]
        s["glu"] = out[9 : 9 + tensor_size]
        terms = scatter_terms(out[9 + tensor_size :])
        s["grad_residual"], s["grad_narrow"], s["inner_mix"] = broad[n].call(
            "grad_residual",
            functools.partial(grad_residual_body, broad[n], full),
            scalars,
            [("rows", cot_rows), ("rows", s["residual"]), ("rows", s["attn"]), ("vec", s["inv2"]), ("vec", total_rows(inner))]
            + [("rows", v) for v in terms],
            [part(width), part(width, NARROW), vec],
        )
    two_kept, two_sent, cot_kept, cot_sent, hidden, grad_gate, grad_up = carried_two

    def weight_term(kept, sent, right):
        return reduce_blocks(
            mm(kept, right, TN).astype(NARROW),
            mm(sent, right, TN).astype(NARROW),
        )

    down_part = weight_term(cot_kept, cot_sent, hidden)
    first_part = weight_term(two_kept, two_sent, grad_gate)
    up_part = weight_term(two_kept, two_sent, grad_up)
    for n in range(chunks):
        s = saved[n]
        shards = gather_shards(s["grad_narrow"])
        inner_mix = total_rows(s["inner_mix"])
        out = tiles[n].call(
            "grad_mix",
            functools.partial(grad_mix_body, tiles[n], full, order),
            scalars,
            [("rows", v) for v in shards]
            + [("rows", s[key]) for key in ("mix", "uz", "qz", "q", "k", "v")]
            + [("state", s["state"]), ("vec", s["square"]), ("vec", inner_mix)]
            + [("whole", v) for v in (inside, start, w_out, finish)],
            full_outs([half_full] * 2 + [width] * 3, carried_three) + [part(width, NARROW), state_shape, vec],
            [pltpu.VMEM((tiles[n].tile, full), NARROW), pltpu.VMEM((tiles[n].tile, width), FLOAT)],
            flops=2 * part_rows * full * width,
        )
        carried_three = out[:5]
        grad_mix, grad_state, inner_one = out[5:]
        grad_update = share_states(grad_state, slopes, span, True)
        out = tiles[n].call(
            "grad_key",
            functools.partial(grad_key_body, tiles[n]),
            scalars,
            [("rows", s["q"]), ("rows", s["k"]), ("rows", s["v"]), ("rows", grad_mix), ("state", grad_update)]
            + [("rows", s["kz"]), ("rows", carried_three[4]), ("rows", carried_three[3]), ("vec", inner_one)]
            + [("whole", v) for v in (inside, finish, w_query, w_key, w_value, w_gate)],
            full_outs([width] * 2, carried_four) + [vec] + pieces,
            [pltpu.VMEM((tiles[n].tile, width), FLOAT)],
            flops=2 * part_rows * full * width * 4,
        )
        carried_four = out[:2]
        s["inner_one"] = out[2]
        s["grad_pieces"] = out[3:]
    out_kept, out_sent, gated, grad_gate_pre, grad_query_pre = carried_three
    out_part = weight_term(out_kept, out_sent, gated)
    one_kept, one_sent = carried_one
    gate_part = weight_term(one_kept, one_sent, grad_gate_pre)
    query_part = weight_term(one_kept, one_sent, grad_query_pre)
    key_part = weight_term(one_kept, one_sent, carried_four[0])
    value_part = weight_term(one_kept, one_sent, carried_four[1])
    output = input_grad = None
    for n in range(chunks):
        s = saved[n]
        output, sums = broad[n].call(
            "output",
            functools.partial(output_body, broad[n]),
            scalars,
            [("rows", s["residual"])] + [("rows", v) for v in scatter_terms(s["glu"])],
            [("rows", (rows, width), NARROW, output), ("acc", (8, width), FLOAT, None)],
        )
        sums_b = sums_b + jnp.sum(sums[0])
        (input_grad,) = broad[n].call(
            "input_grad",
            functools.partial(input_grad_body, broad[n], full),
            scalars,
            [("rows", token_rows), ("rows", s["grad_residual"]), ("vec", s["inv1"]), ("vec", total_rows(s["inner_one"]))]
            + [("rows", v) for v in scatter_terms(s["grad_pieces"])],
            [("rows", (rows, width), NARROW, input_grad)],
        )
    totals = total_rows(jnp.concatenate([sums_a, sums_b[None]]), ("tensor", "dp"))
    token_count = jnp.sum(lengths).astype(FLOAT)
    rms_values = jnp.sqrt(totals / (token_count * full) + EPSILON)
    return (
        output.reshape(tokens.shape),
        input_grad.reshape(tokens.shape),
        query_part,
        key_part,
        value_part,
        gate_part,
        out_part.T,
        jnp.stack([first_part, up_part], axis=1),
        down_part.T,
        rms_values,
    )


def solution(mesh):
    in_specs = (
        P(None, "dp", "tensor"),
        P(None, "dp", "tensor"),
        P(),
        P(None, "tensor"),
        P(None, "tensor"),
        P(None, "tensor"),
        P(None, "tensor"),
        P("tensor", None),
        P(None, None, "tensor"),
        P("tensor", None),
    )
    out_specs = (
        P(None, "dp", "tensor"),
        P(None, "dp", "tensor"),
        P("dp", "tensor"),
        P("dp", "tensor"),
        P("dp", "tensor"),
        P("dp", "tensor"),
        P("tensor", "dp"),
        P("dp", None, "tensor"),
        P("tensor", "dp"),
        P(),
    )
    return jax.shard_map(local, mesh=mesh, in_specs=in_specs, out_specs=out_specs, check_vma=False)
```
